128 devices in a mesh: dp: 16 (over y, x), tensor: 8 (over z, core).
Axes of the slice: x: 4, y: 4, z: 4, core: 2. Of those that a mesh axis runs over, the one named last changes fastest.
Arguments:
- attn_out: bfloat16 [16384, 8192], P('dp', 'tensor'), may hold values from -6 to 6
- out_weight: bfloat16 [8192, 3584], P('tensor', 'dp'), may hold values from -0.0625 to 0.0625
- residual: bfloat16 [16384, 3584], P(('dp', 'tensor')), may hold values from -101 to 101
- norm_gain: float32 [3584], replicated, may hold values from 0.5 to 1.5
- expert_ids: int32 [16384, 8], P(('dp', 'tensor')), may hold values from 0 to 127, all different within a row; in each aligned block of 128 rows (0 to 127, 128 to 255, ...) at most 12 rows name the same one
- route_weight: float32 [16384, 8], P(('dp', 'tensor')), may hold values from 0.05 to 0.35
- w_gate: bfloat16 [128, 3584, 1024], P(('dp', 'tensor')), may hold values from -1 to 1
- w_up: bfloat16 [128, 3584, 1024], P(('dp', 'tensor')), may hold values from -1 to 1
- w_down: bfloat16 [128, 1024, 3584], P(('dp', 'tensor')), may hold values from -0.1875 to 0.1875
- history_x: float32 [16], replicated, may hold values from 8 to 40
- history_h: float32 [16], replicated, may hold values from 4 to 16
Outputs:
- layer_out: bfloat16 [16384, 3584], P(('dp', 'tensor'))
- new_history_x: float32 [16], replicated
- new_history_h: float32 [16], replicated
The draws below stay inside these ranges and needn't reach their ends.
Inputs may be any that keep to these rules, and one draw needn't show every extreme that they name: `expert_ids`: among the routes of one device's 128 tokens no expert is named more than 12 times, a bound that some block reaches.
All inputs are finite; a program needn't handle non-finite values.
Results may differ from the reference program's by a relative error of at most 0.02.
Values may be sent and summed in bfloat16 or wider, within the bound.
A program may use at most 128 MiB of HBM per device.

```python
import math
import jax
import jax.numpy as jnp
import numpy as np
from jax import lax

D = 3584
HEADS = 64
HD = 128
FF = 1024
TOP = 8
HIST = 16
ROWS_DEV = 128
EXPERTS = 128
CAP = 12
TOKENS = 16384
N_TENSOR = 8


def draw_residual(key, part):
    first_key, second_key = jax.random.split(jax.random.fold_in(key, 11))
    ramp = jnp.arange(TOKENS, dtype=jnp.float32)[:, None] / max(TOKENS - 1, 1)
    spread = jnp.clip(jax.random.normal(second_key, (TOKENS, D), jnp.float32), -5.0, 5.0)
    base = jnp.clip(jax.random.normal(first_key, (TOKENS, D), jnp.float32), -5.0, 5.0)
    heavy = 0.15 + 0.45 * ramp
    return (base * jnp.exp(heavy * spread)).astype(jnp.bfloat16)


def rising_weight(key, growth, flat_law):
    ramp = jnp.arange(EXPERTS, dtype=jnp.float32)[:, None, None] / max(EXPERTS - 1, 1)
    factor = D ** (-0.5) * jnp.power(growth, 0.5 * ramp)
    if flat_law:
        values = jax.random.uniform(key, (EXPERTS, D, FF), jnp.float32, -1.7, 1.7)
    else:
        values = jnp.clip(jax.random.normal(key, (EXPERTS, D, FF), jnp.float32), -5.0, 5.0)
    return jnp.clip(values * factor, -1.0, 1.0).astype(jnp.bfloat16)


def draw_w_gate(key, part):
    return rising_weight(jax.random.fold_in(key, 21), 3.0, False)


def draw_w_up(key, part):
    return rising_weight(jax.random.fold_in(key, 37), 3.0, False)


def block_scale(key, shape, pieces, least, high):
    def one(dim, blocks):
        draws = jax.random.uniform(jax.random.fold_in(jax.random.fold_in(key, 6), dim), (blocks,), jnp.float32, least / len(pieces), high / len(pieces))
        return jnp.repeat(jnp.exp(draws), shape[dim] // blocks).reshape((-1,) + (1,) * (len(shape) - dim - 1))

    loudness = one(*pieces[0])
    for cut in pieces[1:]:
        loudness = loudness * one(*cut)
    return loudness


def shared_out(stream_key, own, number, rows, number_of, top, reach, skew):
    sequence = jax.random.permutation(stream_key, number_of)
    heavy_load, common = shares(number_of, rows * top, reach, skew, True), shares(number_of, rows * top, reach, skew, False)
    places = jnp.arange(number_of)

    def named(sizes, offset_by):
        used = int((sizes > 0).sum())
        fixed = max(1, used // 4)
        passed = fixed + (places - fixed + offset_by * (used - fixed)) % max(1, number_of - fixed)
        return jnp.zeros((number_of,), jnp.int32).at[sequence[jnp.where(places < fixed, places, passed)]].set(jnp.asarray(sizes, jnp.int32))

    sizes = jnp.where(number % 4 == 0, named(heavy_load, number // 4), named(common, number - number // 4 - 1))
    mixed = jax.random.permutation(jax.random.fold_in(own, 3), number_of)
    source_of, receiver = mixed[0:number_of // 2 * 2:2], mixed[1:number_of // 2 * 2:2]
    margin = jnp.minimum(sizes[source_of] - 1, reach - sizes[receiver]) // 2
    margin = jnp.where((source_of == sequence[0]) | (receiver == sequence[0]) | (sizes[receiver] == 0), 0, jnp.maximum(margin, 0))
    passed = jax.random.randint(jax.random.fold_in(own, 4), (number_of // 2,), 0, 1 << 20) % (margin + 1)
    sizes = sizes.at[source_of].add(-passed).at[receiver].add(passed)
    labels = jnp.searchsorted(jnp.cumsum(sizes), jnp.arange(rows * top), side="right").astype(jnp.int32)
    grid = labels.reshape(top, rows).T
    grid = grid[jax.random.permutation(jax.random.fold_in(own, 1), rows)]
    offset_by = jax.random.randint(jax.random.fold_in(own, 2), (rows, 1), 0, top)
    return jnp.take_along_axis(grid, (jnp.arange(top)[None, :] + offset_by) % top, axis=1)


def shares(number_of, total, reach, slope, full):
    weights = [(1 << 20) // math.isqrt(grade ** slope) + 1 for grade in range(1, number_of + 1)]
    largest = reach if full else min(reach, max(-(-total // number_of), total * weights[0] // sum(weights)))
    least = 1 if total - largest >= number_of - 1 else 0
    counts, rest = [largest] + [least] * (number_of - 1), total - largest - least * (number_of - 1)
    while rest > 0:
        candidates = [i for i in range(1, number_of) if counts[i] < largest] or [i for i in range(1, number_of) if counts[i] < reach]
        whole, left = sum([weights[i] for i in candidates]), rest
        for i in candidates:
            extra = min(reach - counts[i], max(1, left * weights[i] // whole), rest)
            counts[i] = counts[i] + extra
            rest = rest - extra
    return np.array(counts)


def scatter_about(stream_key, shape, deviation, most, cuts=(), kind=jnp.bfloat16):
    result = jax.random.normal(stream_key, shape, jnp.float32) * deviation
    if len(cuts) > 0:
        result = block_scale(stream_key, shape, cuts, -0.22, 0.18) * result
    return jnp.clip(result, min=-most, max=most).astype(kind)


def setup_inputs(seed: int = 0) -> dict:
    streams_of = jax.random.split(jax.random.key(seed), 12)
    attn_out = scatter_about(streams_of[0], (TOKENS, HEADS * HD), 1.0, 6.0, ((0, 16), (1, 8)))
    out_weight = scatter_about(streams_of[1], (HEADS * HD, D), (HEADS * HD) ** -0.5, 0.0625, ((0, 8), (1, 16)))
    residual = draw_residual(jax.random.fold_in(streams_of[11], 71), 0)
    norm_gain = jnp.clip(1.0 + 0.1 * jax.random.normal(streams_of[3], (D,), jnp.float32), 0.5, 1.5)
    expert_ids_keys = jax.random.split(jax.random.fold_in(streams_of[4], 1), TOKENS // ROWS_DEV)
    expert_ids_turns = jax.random.permutation(jax.random.fold_in(streams_of[4], 3), TOKENS // ROWS_DEV)
    expert_ids = jax.vmap(lambda own, number: shared_out(jax.random.fold_in(streams_of[4], 2), own, number, ROWS_DEV, EXPERTS, TOP, CAP, 2))(expert_ids_keys, expert_ids_turns).reshape((TOKENS, TOP))
    route_weight = jnp.clip(0.05 + 0.29999999 * jax.random.uniform(streams_of[5], (TOKENS, TOP), jnp.float32) ** block_scale(streams_of[5], (TOKENS, TOP), ((0, 128),), -0.2, 0.2), 0.05, 0.35)
    w_gate = draw_w_gate(jax.random.fold_in(streams_of[11], 71), 0)
    w_up = draw_w_up(jax.random.fold_in(streams_of[11], 71), 0)
    w_down = scatter_about(streams_of[8], (EXPERTS, FF, D), FF ** -0.5, 0.1875, ((0, 128),))
    history_x = jnp.clip(jnp.exp(jax.random.uniform(streams_of[9], (HIST,), jnp.float32, math.log(8.0), math.log(40.0))), 8.0, 40.0)
    history_h = jnp.clip(jnp.exp(jax.random.uniform(streams_of[10], (HIST,), jnp.float32, math.log(4.0), math.log(16.0))), 4.0, 16.0)
    return dict(attn_out=attn_out, out_weight=out_weight, residual=residual, norm_gain=norm_gain, expert_ids=expert_ids, route_weight=route_weight, w_gate=w_gate, w_up=w_up, w_down=w_down, history_x=history_x, history_h=history_h)


FP8_LIMIT = 448.0

def reference(attn_out, out_weight, residual, norm_gain, expert_ids, route_weight, w_gate, w_up, w_down, history_x, history_h):
    block_width = HEADS * HD // N_TENSOR
    projected = jnp.zeros((TOKENS, D), jnp.float32)
    for column_block in range(N_TENSOR):
        lower = column_block * block_width
        partial_sum = jnp.dot(attn_out[:, lower:lower + block_width], out_weight[lower:lower + block_width], preferred_element_type=jnp.float32)
        rounded = lax.optimization_barrier(partial_sum.astype(jnp.bfloat16))
        projected = projected + rounded.astype(jnp.float32)
    stream = residual.astype(jnp.float32) + projected
    normed = stream * lax.rsqrt(lax.optimization_barrier(jnp.mean(stream * stream, axis=-1, keepdims=True)) + 1e-06) * norm_gain
    amax_x = jnp.max(jnp.abs(normed))
    scale_x = FP8_LIMIT / jnp.max(history_x)
    inv_x = jnp.max(history_x) / FP8_LIMIT
    scale_h = FP8_LIMIT / jnp.max(history_h)
    inv_h = jnp.max(history_h) / FP8_LIMIT
    quantized = jnp.clip(normed * scale_x, -FP8_LIMIT, FP8_LIMIT).astype(jnp.bfloat16)
    sources = TOKENS // ROWS_DEV
    flat_ids = expert_ids.reshape(sources, ROWS_DEV * TOP)
    onehot = (flat_ids[:, :, None] == jnp.arange(EXPERTS, dtype=jnp.int32)[None, None, :]).astype(jnp.int32)
    before = jnp.cumsum(onehot, axis=1) - onehot
    slot_index = lax.optimization_barrier(jnp.sum(before * onehot, axis=-1))
    position = flat_ids * (sources * CAP) + jnp.arange(sources, dtype=jnp.int32)[:, None] * CAP + slot_index
    table = jnp.full((EXPERTS * sources * CAP,), -1, jnp.int32)
    table = table.at[position.reshape(-1)].set(jnp.arange(TOKENS * TOP, dtype=jnp.int32))
    table = table.reshape(EXPERTS, sources * CAP)
    flat_weight = route_weight.reshape(-1)

    def one_expert(carry, inputs):
        running, largest = carry
        gate_matrix, up_matrix, down_matrix, entries = inputs
        valid = entries >= 0
        safe_entry = jnp.where(valid, entries, 0)
        token_index = safe_entry // TOP
        picked = quantized[token_index]
        picked = jnp.where(valid[:, None], picked, jnp.zeros_like(picked))
        gate = jnp.dot(picked, gate_matrix, preferred_element_type=jnp.float32) * inv_x
        upper = jnp.dot(picked, up_matrix, preferred_element_type=jnp.float32) * inv_x
        hidden = jax.nn.silu(gate) * upper
        largest = jnp.maximum(largest, jnp.max(jnp.abs(hidden)))
        hidden_q = jnp.clip(hidden * scale_h, -FP8_LIMIT, FP8_LIMIT).astype(jnp.bfloat16)
        expert_out = (jnp.dot(hidden_q, down_matrix, preferred_element_type=jnp.float32) * inv_h).astype(jnp.bfloat16)
        weights = jnp.where(valid, flat_weight[safe_entry], jnp.zeros((), jnp.float32))
        running = running.at[token_index].add(expert_out.astype(jnp.float32) * weights[:, None])
        return ((running, largest), None)
    start_carry = (jnp.zeros((TOKENS, D), jnp.float32), jnp.zeros((), jnp.float32))
    (mixture, amax_h), _ = lax.scan(one_expert, start_carry, (w_gate, w_up, w_down, table))
    layer_out = (stream + mixture).astype(jnp.bfloat16)
    new_history_x = jnp.concatenate([amax_x[None], history_x[:-1]])
    new_history_h = jnp.concatenate([amax_h[None], history_h[:-1]])
    return (layer_out, new_history_x, new_history_h)
```

```python
import jax
import jax.numpy as jnp
from jax import lax
from jax.sharding import Mesh
from jax.sharding import PartitionSpec as P

FP8_LIMIT = 448.0
CHIPS = ("dp", "z")
ALL = ("dp", "z", "core")
SWAP = [(0, 1), (1, 0)]


def body(
    attn_out,
    out_weight,
    residual,
    norm_gain,
    expert_ids,
    route_weight,
    w_gate,
    w_up,
    w_down,
    history_x,
    history_h,
):
    chips = lax.axis_size("dp") * lax.axis_size("z")
    experts = 2 * chips
    core = lax.axis_index("core")
    rows = residual.shape[0]
    width = residual.shape[1]
    top = expert_ids.shape[1]
    cap = max(2, 3 * rows * top // (2 * experts))
    block = 2 * cap
    slots = chips * block

    chosen = expert_ids[:, :, None] == jnp.arange(experts, dtype=jnp.int32)[None, None, :]
    member = jnp.sum(chosen.astype(jnp.float32), axis=1)
    earlier = (
        lax.broadcasted_iota(jnp.int32, (rows, rows), 1)
        < lax.broadcasted_iota(jnp.int32, (rows, rows), 0)
    ).astype(jnp.bfloat16)
    before = jnp.dot(earlier, member.astype(jnp.bfloat16), preferred_element_type=jnp.float32)
    rank = (before + 1.0) * member
    gain = jnp.sum(jnp.where(chosen, route_weight[:, :, None], 0.0), axis=1)
    table = jnp.stack([rank, gain]).astype(jnp.bfloat16)
    other_table = lax.ppermute(table, "core", SWAP)
    table = jnp.concatenate([table, other_table], axis=1)

    column = lax.broadcasted_iota(jnp.int32, (experts, slots), 1)
    spread = (
        lax.broadcasted_iota(jnp.int32, (experts, slots), 0) == 2 * (column // block) + core
    ).astype(jnp.bfloat16)
    spread_rank = jnp.dot(table[0], spread, preferred_element_type=jnp.float32)
    spread_gain = jnp.dot(table[1], spread, preferred_element_type=jnp.float32)
    column = lax.broadcasted_iota(jnp.int32, (2 * rows, slots), 1)
    source = lax.broadcasted_iota(jnp.int32, (2 * rows, slots), 0) // rows
    source = jnp.where(core == 0, source, 1 - source)
    hit = (spread_rank == (column % cap + 1).astype(jnp.float32)) & ((column // cap) % 2 == source)
    placing = hit.astype(jnp.bfloat16)
    mixing = jnp.where(hit, spread_gain, 0.0).astype(jnp.bfloat16)

    head_terms = jnp.dot(
        attn_out,
        lax.all_gather(out_weight, "dp", axis=1, tiled=True),
        preferred_element_type=jnp.float32,
    )
    projected = lax.psum_scatter(
        head_terms.astype(jnp.bfloat16), ("z", "core"), scatter_dimension=0, tiled=True
    ).astype(jnp.float32)
    stream = residual.astype(jnp.float32) + projected
    normed = (
        stream * lax.rsqrt(jnp.mean(stream * stream, axis=-1, keepdims=True) + 1e-06) * norm_gain
    )
    peak_x = jnp.max(jnp.abs(normed))
    scale_x = FP8_LIMIT / jnp.max(history_x)
    inv_x = jnp.max(history_x) / FP8_LIMIT
    scale_h = FP8_LIMIT / jnp.max(history_h)
    inv_h = jnp.max(history_h) / FP8_LIMIT
    quantized = jnp.clip(normed * scale_x, -FP8_LIMIT, FP8_LIMIT).astype(jnp.bfloat16)
    quantized = jnp.concatenate([quantized, lax.ppermute(quantized, "core", SWAP)], axis=0)
    outgoing = lax.dot_general(
        placing, quantized, (((0,), (0,)), ((), ())), preferred_element_type=jnp.float32
    )
    outgoing = outgoing.astype(jnp.bfloat16).reshape(chips, block, width)
    tokens = lax.all_to_all(outgoing, CHIPS, split_axis=0, concat_axis=0, tiled=True)
    tokens = tokens.reshape(slots, width)

    gate = jnp.dot(tokens, w_gate[0], preferred_element_type=jnp.float32) * inv_x
    upper = jnp.dot(tokens, w_up[0], preferred_element_type=jnp.float32) * inv_x
    hidden = jax.nn.silu(gate) * upper
    peak_h = jnp.max(jnp.abs(hidden))
    lane = lax.broadcasted_iota(jnp.int32, (chips, 8, 128), 1)
    peaks = lax.all_to_all(
        jnp.where(lane == 0, peak_x, peak_h), CHIPS, split_axis=0, concat_axis=0, tiled=True
    )
    hidden_q = jnp.clip(hidden * scale_h, -FP8_LIMIT, FP8_LIMIT).astype(jnp.bfloat16)
    expert_out = (
        jnp.dot(hidden_q, w_down[0], preferred_element_type=jnp.float32) * inv_h
    ).astype(jnp.bfloat16)
    expert_out, peaks = lax.optimization_barrier((expert_out, peaks))
    peaks = jnp.max(peaks, axis=0)
    peaks = jnp.maximum(peaks, lax.ppermute(peaks, "core", SWAP))
    returned = lax.all_to_all(
        expert_out.reshape(chips, block, width), CHIPS, split_axis=0, concat_axis=0, tiled=True
    ).reshape(slots, width)
    for_other = jnp.dot(mixing[rows:], returned, preferred_element_type=jnp.float32)
    from_other = lax.ppermute(for_other.astype(jnp.bfloat16), "core", SWAP)
    mixture = jnp.dot(mixing[:rows], returned, preferred_element_type=jnp.float32)
    layer_out = (stream + mixture + from_other.astype(jnp.float32)).astype(jnp.bfloat16)
    new_history_x = jnp.concatenate([peaks[0, :1], history_x[:-1]])
    new_history_h = jnp.concatenate([peaks[1, :1], history_h[:-1]])
    return (layer_out, new_history_x, new_history_h)


def solution(mesh):
    dp, tensor = mesh.shape["dp"], mesh.shape["tensor"]
    fine = Mesh(mesh.devices.reshape(dp, tensor // 2, 2), ALL)
    in_specs = (
        P("dp", ("z", "core")),
        P(("z", "core"), "dp"),
        P(ALL, None),
        P(),
        P(ALL, None),
        P(ALL, None),
        P(ALL, None, None),
        P(ALL, None, None),
        P(ALL, None, None),
        P(),
        P(),
    )
    out_specs = (P(ALL, None), P(), P())
    return jax.shard_map(body, mesh=fine, in_specs=in_specs, out_specs=out_specs, check_vma=False)
```

```python
import jax
import jax.numpy as jnp
from jax import lax
from jax.experimental import pallas as pl
from jax.experimental.pallas import tpu as pltpu
from jax.sharding import Mesh
from jax.sharding import PartitionSpec as P

FP8_LIMIT = 448.0
DP = ("y", "x")
CHIPS = ("y", "x", "z")
ALL = ("y", "x", "z", "core")
RING = 4
TURNS = (1, 3, 2)
SWAP = [(0, 1), (1, 0)]


def project_kernel(
    a_ref,
    w_ref,
    out_ref,
    gathered,
    pair_out,
    pair_in,
    own,
    sums,
    arrived,
    total,
    near_sem,
    relay_sem,
    gathered_sem,
    pair_send,
    pair_recv,
    sum_send,
    sum_recv,
):
    y, x, z, core = (lax.axis_index(name) for name in ALL)
    shards, _, half_depth, inner = gathered.shape
    depth = 2 * half_depth
    token = a_ref.shape[2]

    def step(position, turn):
        return lax.rem(position + turn, RING)

    def along(axis, turn):
        if axis == "x":
            return (y, step(x, turn), z, core)
        if axis == "y":
            return (step(y, turn), x, z, core)
        return (y, x, step(z, turn), core)

    sibling = (y, x, z, 1 - core)
    mesh_id = pl.DeviceIdType.MESH

    def copy(src, dst, send, recv, device):
        return pltpu.make_async_remote_copy(
            src_ref=src,
            dst_ref=dst,
            send_sem=send,
            recv_sem=recv,
            device_id=device,
            device_id_type=mesh_id,
        )

    barrier = pltpu.get_barrier_semaphore()
    for axis in ("x", "y", "z"):
        for turn in TURNS:
            pl.semaphore_signal(
                barrier, inc=1, device_id=along(axis, turn), device_id_type=mesh_id
            )
    pl.semaphore_signal(barrier, inc=1, device_id=sibling, device_id_type=mesh_id)
    pl.semaphore_wait(barrier, 10)

    mine = y * RING + x

    def near(number, half, axis):
        return copy(
            w_ref.at[half],
            gathered.at[mine, half],
            near_sem.at[half, 0 if axis == "x" else 1, number],
            gathered_sem.at[mine, half],
            along(axis, TURNS[number]),
        )

    for number in range(3):
        near(number, 0, "x").start()
        near(number, 1, "y").start()

    def arrival(shard, half):
        return copy(
            gathered.at[shard, half],
            gathered.at[shard, half],
            near_sem.at[0, 0, 0],
            gathered_sem.at[shard, half],
            sibling,
        )

    def shard_at(turn_y, turn_x):
        return step(y, turn_y) * RING + step(x, turn_x)

    def relay(half, source, number):
        shard = shard_at(0, source) if half == 0 else shard_at(source, 0)
        return copy(
            gathered.at[shard, half],
            gathered.at[shard, half],
            relay_sem.at[half, source - 1, number],
            gathered_sem.at[shard, half],
            along("y" if half == 0 else "x", TURNS[number]),
        )

    def to_sibling(i):
        return copy(pair_out.at[i], pair_in.at[i], pair_send.at[i], pair_recv.at[i], sibling)

    def to_owner(i, turn):
        return copy(
            sums.at[i, step(z, turn)],
            arrived.at[i, turn - 1],
            sum_send.at[i, turn - 1],
            sum_recv.at[i, turn - 1],
            along("z", turn),
        )

    def terms(block, which):
        rows = a_ref[:, which].reshape(RING * token, inner)
        return lax.dot_general(
            block, rows, (((1,), (1,)), ((), ())), preferred_element_type=jnp.float32
        )

    def share(i, block):
        pair_out[i] = terms(block, 1 - core).astype(jnp.bfloat16)
        to_sibling(i).start()

    def send_sums(i):
        to_sibling(i).wait_recv()
        both = (own[lax.rem(i, 2)] + pair_in[i].astype(jnp.float32)).astype(jnp.bfloat16)
        for part in range(RING):
            sums[i, part] = both[:, part * token : (part + 1) * token]
        for turn in TURNS:
            to_owner(i, turn).start()

    def advance(i, shard):
        block = gathered[shard].reshape(depth, inner)
        share(i, block)
        send_sums(i - 1)
        own[lax.rem(i, 2)] = terms(block, core)

    def collect(i, shard):
        for turn in TURNS:
            to_owner(i, turn).wait_recv()
        value = sums[i, z].astype(jnp.float32)
        for turn in TURNS:
            value = value + arrived[i, turn - 1].astype(jnp.float32)
        total[pl.ds(pl.multiple_of(shard * depth, 8), depth), :] = value

    def turn_of(j):
        return 1 + 2 * j - 3 * (j // 2)

    block = w_ref[...].reshape(depth, inner)
    share(0, block)
    for number in range(3):
        near(number, 0, "y").start()
        near(number, 1, "x").start()
    own[0] = terms(block, core)
    for source in TURNS:
        arrival(shard_at(0, source), 0).wait_recv()
        for number in range(3):
            relay(0, source, number).start()
        arrival(shard_at(source, 0), 1).wait_recv()
        for number in range(3):
            relay(1, source, number).start()

    def straight(j, carry):
        turn = turn_of(j)
        shard = shard_at(0, turn)
        arrival(shard, 1).wait_recv()
        advance(1 + 2 * j, shard)
        shard = shard_at(turn, 0)
        arrival(shard, 0).wait_recv()
        advance(2 + 2 * j, shard)
        return carry

    lax.fori_loop(0, 3, straight, 0)

    collect(0, mine)

    def collect_straight(j):
        turn = turn_of(j)
        collect(1 + 2 * j, shard_at(0, turn))
        collect(2 + 2 * j, shard_at(turn, 0))

    def diagonal_shard(j):
        return shard_at(turn_of(j // 3), turn_of(lax.rem(j, 3)))

    def diagonal(j, carry):
        shard = diagonal_shard(j)
        arrival(shard, 0).wait_recv()
        arrival(shard, 1).wait_recv()
        advance(7 + j, shard)

        @pl.when(lax.rem(j, 3) == 2)
        def _():
            collect_straight(j // 3)

        return carry

    lax.fori_loop(0, 9, diagonal, 0)
    send_sums(shards - 1)

    def collect_diagonal(j, carry):
        collect(7 + j, diagonal_shard(j))
        return carry

    lax.fori_loop(0, 9, collect_diagonal, 0)

    def turn_over(b, carry):
        start = pl.multiple_of(b * token, token)
        out_ref[:, pl.ds(start, token)] = total[pl.ds(start, token), :].T
        return carry

    lax.fori_loop(0, total.shape[0] // token, turn_over, 0)

    for number in range(3):
        for half in range(2):
            near(number, half, "x").wait_send()
            near(number, half, "y").wait_send()
            for source in TURNS:
                relay(half, source, number).wait_send()

    def finish(i, carry):
        to_sibling(i).wait_send()
        for turn in TURNS:
            to_owner(i, turn).wait_send()
        return carry

    lax.fori_loop(0, shards, finish, 0)


def project(attn_out, out_weight):
    inner, depth = out_weight.shape
    shards = RING * RING
    token = attn_out.shape[0] // (2 * RING)
    width = shards * depth
    vmem = pl.BlockSpec(memory_space=pltpu.VMEM)
    dma = pltpu.SemaphoreType.DMA
    return pl.pallas_call(
        project_kernel,
        out_shape=jax.ShapeDtypeStruct((token, width), jnp.float32),
        in_specs=[vmem, vmem],
        out_specs=vmem,
        scratch_shapes=[
            pltpu.VMEM((shards, 2, depth // 2, inner), jnp.bfloat16),
            pltpu.VMEM((shards, depth, RING * token), jnp.bfloat16),
            pltpu.VMEM((shards, depth, RING * token), jnp.bfloat16),
            pltpu.VMEM((2, depth, RING * token), jnp.float32),
            pltpu.VMEM((shards, RING, depth, token), jnp.bfloat16),
            pltpu.VMEM((shards, RING - 1, depth, token), jnp.bfloat16),
            pltpu.VMEM((width, token), jnp.float32),
            dma((2, 2, 3)),
            dma((2, 3, 3)),
            dma((shards, 2)),
            dma((shards,)),
            dma((shards,)),
            dma((shards, 3)),
            dma((shards, 3)),
        ],
        compiler_params=pltpu.CompilerParams(
            collective_id=0, has_side_effects=True, vmem_limit_bytes=48 << 20
        ),
        cost_estimate=pl.CostEstimate(
            flops=2 * attn_out.shape[0] * inner * width,
            bytes_accessed=2 * attn_out.size + 2 * out_weight.size + 4 * token * width,
            transcendentals=0,
        ),
        name="project",
    )(attn_out.reshape(RING, 2, token, inner), out_weight.T.reshape(2, depth // 2, inner))


def body(
    attn_out,
    out_weight,
    residual,
    norm_gain,
    expert_ids,
    route_weight,
    w_gate,
    w_up,
    w_down,
    history_x,
    history_h,
):
    chips = lax.axis_size(CHIPS)
    experts = 2 * chips
    core = lax.axis_index("core")
    rows = residual.shape[0]
    width = residual.shape[1]
    top = expert_ids.shape[1]
    cap = max(2, 3 * rows * top // (2 * experts))
    block = 2 * cap
    slots = chips * block

    chosen = expert_ids[:, :, None] == jnp.arange(experts, dtype=jnp.int32)[None, None, :]
    member = jnp.sum(chosen.astype(jnp.float32), axis=1)
    earlier = (
        lax.broadcasted_iota(jnp.int32, (rows, rows), 1)
        < lax.broadcasted_iota(jnp.int32, (rows, rows), 0)
    ).astype(jnp.bfloat16)
    before = jnp.dot(earlier, member.astype(jnp.bfloat16), preferred_element_type=jnp.float32)
    rank = (before + 1.0) * member
    gain = jnp.sum(jnp.where(chosen, route_weight[:, :, None], 0.0), axis=1)
    table = jnp.stack([rank, gain]).astype(jnp.bfloat16)
    other_table = lax.ppermute(table, "core", SWAP)
    table = jnp.concatenate([table, other_table], axis=1)

    column = lax.broadcasted_iota(jnp.int32, (experts, slots), 1)
    spread = (
        lax.broadcasted_iota(jnp.int32, (experts, slots), 0) == 2 * (column // block) + core
    ).astype(jnp.bfloat16)
    spread_rank = jnp.dot(table[0], spread, preferred_element_type=jnp.float32)
    spread_gain = jnp.dot(table[1], spread, preferred_element_type=jnp.float32)
    column = lax.broadcasted_iota(jnp.int32, (2 * rows, slots), 1)
    source = lax.broadcasted_iota(jnp.int32, (2 * rows, slots), 0) // rows
    source = jnp.where(core == 0, source, 1 - source)
    hit = (spread_rank == (column % cap + 1).astype(jnp.float32)) & ((column // cap) % 2 == source)
    placing = hit.astype(jnp.bfloat16)
    mixing = jnp.where(hit, spread_gain, 0.0).astype(jnp.bfloat16)

    projected = project(attn_out, out_weight)
    stream = residual.astype(jnp.float32) + projected
    normed = (
        stream * lax.rsqrt(jnp.mean(stream * stream, axis=-1, keepdims=True) + 1e-06) * norm_gain
    )
    peak_x = jnp.max(jnp.abs(normed))
    scale_x = FP8_LIMIT / jnp.max(history_x)
    inv_x = jnp.max(history_x) / FP8_LIMIT
    scale_h = FP8_LIMIT / jnp.max(history_h)
    inv_h = jnp.max(history_h) / FP8_LIMIT
    quantized = jnp.clip(normed * scale_x, -FP8_LIMIT, FP8_LIMIT).astype(jnp.bfloat16)
    quantized = jnp.concatenate([quantized, lax.ppermute(quantized, "core", SWAP)], axis=0)
    outgoing = lax.dot_general(
        placing, quantized, (((0,), (0,)), ((), ())), preferred_element_type=jnp.float32
    )
    outgoing = outgoing.astype(jnp.bfloat16).reshape(chips, block, width)
    tokens = lax.all_to_all(outgoing, CHIPS, split_axis=0, concat_axis=0, tiled=True)
    tokens = tokens.reshape(slots, width)

    gate = jnp.dot(tokens, w_gate[0], preferred_element_type=jnp.float32) * inv_x
    upper = jnp.dot(tokens, w_up[0], preferred_element_type=jnp.float32) * inv_x
    hidden = jax.nn.silu(gate) * upper
    peak_h = jnp.max(jnp.abs(hidden))
    lane = lax.broadcasted_iota(jnp.int32, (8, 128), 0)
    peaks = lax.optimization_barrier(jnp.where(lane == 0, peak_x, peak_h))
    peaks = lax.optimization_barrier(lax.all_gather(peaks, ALL))
    mixing, peaks = lax.optimization_barrier((mixing, jnp.max(peaks, axis=0)))
    hidden_q = jnp.clip(hidden * scale_h, -FP8_LIMIT, FP8_LIMIT).astype(jnp.bfloat16)
    expert_out = (
        jnp.dot(hidden_q, w_down[0], preferred_element_type=jnp.float32) * inv_h
    ).astype(jnp.bfloat16)
    returned = lax.all_to_all(
        expert_out.reshape(chips, block, width), CHIPS, split_axis=0, concat_axis=0, tiled=True
    ).reshape(slots, width)
    for_other = jnp.dot(mixing[rows:], returned, preferred_element_type=jnp.float32)
    from_other = lax.ppermute(for_other.astype(jnp.bfloat16), "core", SWAP)
    mixture = jnp.dot(mixing[:rows], returned, preferred_element_type=jnp.float32)
    layer_out = (stream + mixture + from_other.astype(jnp.float32)).astype(jnp.bfloat16)
    new_history_x = jnp.concatenate([peaks[0, :1], history_x[:-1]])
    new_history_h = jnp.concatenate([peaks[1, :1], history_h[:-1]])
    return (layer_out, new_history_x, new_history_h)


def solution(mesh):
    fine = Mesh(mesh.devices.reshape(RING, RING, RING, 2), ALL)
    in_specs = (
        P(DP, ("z", "core")),
        P(("z", "core"), DP),
        P(ALL, None),
        P(),
        P(ALL, None),
        P(ALL, None),
        P(ALL, None, None),
        P(ALL, None, None),
        P(ALL, None, None),
        P(),
        P(),
    )
    out_specs = (P(ALL, None), P(), P())
    return jax.shard_map(body, mesh=fine, in_specs=in_specs, out_specs=out_specs, check_vma=False)
```
